128 devices in a mesh: dp: 8 (over y, core), tensor: 16 (over z, x).
Axes of the slice: x: 4, y: 4, z: 4, core: 2. Of those that a mesh axis runs over, the one named last changes fastest.
Arguments:
- thinker_rows: bfloat16 [16384, 8192], P('dp', 'tensor'), may hold values from -6 to 6
- proj_weight: bfloat16 [8192, 3584], P('tensor'), may hold values from -0.0625 to 0.0625
- proj_bias: float32 [3584], replicated, may hold values from -3 to 3
- cotangent: bfloat16 [16384, 3584], P('dp'), may hold values from -6 to 6
- block_owner: int32 [128], P('dp'), may hold values from 0 to 7, as said below
- block_offset: int32 [128], P('dp'), may hold values from 0 to 31, as said below
Outputs:
- grad_thinker: bfloat16 [32768, 8192], P('dp', 'tensor')
- proj_grad: float32 [8192, 3584], P(('tensor', 'dp'))
The draws below stay inside these ranges and needn't reach their ends.
Inputs may be any that keep to these rules, and one draw needn't show every extreme that they name: `block_owner`: the 16 blocks of one index of dp name at most 4 blocks for any one owner, and the blocks for one owner stand next to each other; one owner receives exactly 4 blocks from every index of dp. `block_offset`: no two talker blocks share both owner and offset.
All inputs are finite; a program needn't handle non-finite values.
Results may differ from the reference program's by a relative error of at most 0.015.
Values may be sent and summed in bfloat16 or wider, within the bound.
A program may use at most 128 MiB of HBM per device.

```python
import jax
import jax.numpy as jnp
from jax import lax

D = 8192
E = 3584
BLOCK = 128
BLK_DEV = 16
OWN_BLK = 32
BLOCKS = 128
TOKENS = 16384
N_DP = 8
N_TENSOR = 16


def routing_tables(key):
    slot_cap = 2 * BLK_DEV // N_DP
    heavy_owner = jax.random.randint(jax.random.fold_in(key, 11), (), 0, N_DP)
    tickets = jnp.repeat(jnp.arange(N_DP, dtype=jnp.int32), slot_cap)

    def one_source(source):
        source_key = jax.random.fold_in(key, 100 + source)
        ticket_noise = jax.random.permutation(jax.random.fold_in(source_key, 1), tickets.shape[0]).astype(jnp.int32)
        ticket_score = jnp.where(tickets == heavy_owner, 0, 1 + ticket_noise)
        chosen = tickets[jnp.argsort(ticket_score)[:BLK_DEV]]
        owner_rank = jax.random.permutation(jax.random.fold_in(source_key, 2), N_DP).astype(jnp.int32)
        grouping = owner_rank[chosen] * BLK_DEV + jnp.arange(BLK_DEV, dtype=jnp.int32)
        return chosen[jnp.argsort(grouping)]
    owners = jax.vmap(one_source)(jnp.arange(N_DP, dtype=jnp.int32))
    owner_hot = (owners[:, :, None] == jnp.arange(N_DP, dtype=jnp.int32)[None, None, :]).astype(jnp.int32)
    within = jnp.sum((jnp.cumsum(owner_hot, axis=1) - owner_hot) * owner_hot, axis=2)
    linear = jnp.arange(N_DP, dtype=jnp.int32)[:, None] * slot_cap + within

    def one_shuffle(owner):
        return jax.random.permutation(jax.random.fold_in(key, 500 + owner), 2 * BLK_DEV).astype(jnp.int32)
    shuffles = jax.vmap(one_shuffle)(jnp.arange(N_DP, dtype=jnp.int32))
    offsets = shuffles[owners, linear]
    return (owners.reshape(-1).astype(jnp.int32), offsets.reshape(-1).astype(jnp.int32))


def draw_block_owner(key, part):
    return routing_tables(key)[0]


def draw_block_offset(key, part):
    return routing_tables(key)[1]


def spiked(drawn, rng, source, target, parts, factor):
    owner, partner = [(jnp.arange(drawn.shape[position]) // (drawn.shape[position] // parts)).reshape([-1 if axis == position else 1 for axis in range(drawn.ndim)]) for position in (source, target)]
    chosen = jax.random.permutation(rng, parts)[partner]
    strong = (owner == chosen) | (owner == (partner + parts // 2) % parts)
    return jnp.where(strong, factor * drawn, drawn)


def steps_of(stream_key, dims, shards, smallest, top_value):
    def one(dim, parts):
        draws = jax.random.uniform(jax.random.fold_in(jax.random.fold_in(stream_key, 6), dim), (parts,), jnp.float32, smallest / len(shards), top_value / len(shards))
        return jnp.repeat(jnp.exp(draws), dims[dim] // parts).reshape((-1,) + (1,) * (len(dims) - dim - 1))

    loudness = one(*shards[0])
    for cut in shards[1:]:
        loudness = loudness * one(*cut)
    return loudness


def centred(stream_key, dims, width, bound, pieces=(), held_as=jnp.bfloat16):
    array = jax.random.normal(stream_key, dims, jnp.float32) * width
    if len(pieces) > 0:
        array = steps_of(stream_key, dims, pieces, -0.22, 0.18) * array
    return jnp.clip(array, min=-bound, max=bound).astype(held_as)


def bell_draw_with(own_key, shape, spread, limit, cuts, heavy, held_as=jnp.bfloat16):
    drawn = spread * jax.random.normal(own_key, shape, jnp.float32)
    if cuts:
        drawn = drawn * steps_of(own_key, shape, cuts, -0.22, 0.18)
    return jnp.clip(spiked(drawn, jax.random.fold_in(own_key, 3), *heavy), -limit, limit).astype(held_as)


def setup_inputs(seed: int = 0) -> dict:
    key_list = jax.random.split(jax.random.key(seed), 7)
    return {
        "thinker_rows": bell_draw_with(key_list[0], (TOKENS, D), 1.0, 6.0, ((0, 8), (1, 16)), (0, 1, 16, 2.0)),
        "proj_weight": centred(key_list[1], (D, E), D ** -0.5, 0.0625, ((0, 16),)),
        "proj_bias": centred(key_list[2], (E,), 1.0, 3.0, (), jnp.float32),
        "cotangent": centred(key_list[3], (TOKENS, E), 1.0, 6.0, ((0, 8),)),
        "block_owner": draw_block_owner(jax.random.fold_in(key_list[6], 71), 0),
        "block_offset": draw_block_offset(jax.random.fold_in(key_list[6], 71), 0),
    }


def reference(thinker_rows, proj_weight, proj_bias, cotangent, block_owner, block_offset):
    local_width = D // N_TENSOR
    stacked_rows = thinker_rows.reshape(TOKENS, N_TENSOR, local_width).transpose(1, 0, 2)
    stacked_weight = proj_weight.reshape(N_TENSOR, local_width, E)

    def add_part(total, pair):
        partial_value = jnp.dot(pair[0], pair[1], preferred_element_type=jnp.float32)
        rounded = lax.optimization_barrier(partial_value.astype(jnp.bfloat16))
        return total + rounded.astype(jnp.float32), None

    summed, _ = lax.scan(add_part, jnp.zeros((TOKENS, E), jnp.float32), (stacked_rows, stacked_weight))
    pre_act = summed + proj_bias
    gate_value = jax.nn.sigmoid(pre_act)
    slope_rows = (cotangent.astype(jnp.float32) * gate_value * (1.0 + pre_act * (1.0 - gate_value))).astype(jnp.bfloat16)
    input_grad = jnp.dot(slope_rows, proj_weight.T, preferred_element_type=jnp.float32).astype(jnp.bfloat16)
    proj_grad = jnp.dot(thinker_rows.T, slope_rows, preferred_element_type=jnp.float32) * (TOKENS ** -0.5)
    target = (block_owner.astype(jnp.int32) * OWN_BLK + block_offset.astype(jnp.int32)).astype(jnp.int32)
    owner_grad = jnp.zeros((N_DP * OWN_BLK, BLOCK, D), jnp.bfloat16)
    owner_grad = owner_grad.at[target].set(input_grad.reshape(BLOCKS, BLOCK, D))
    return owner_grad.reshape(N_DP * OWN_BLK * BLOCK, D), proj_grad
```

```python
import jax
import jax.numpy as jnp
from jax import lax
from jax.experimental import pallas as pl
from jax.experimental.pallas import tpu as pltpu
from jax.sharding import PartitionSpec as P

BLOCK = 128
CHUNKS = 4


def slope_of(summed, proj_bias, cot_rows):
    pre_act = summed + proj_bias
    gate_value = jax.nn.sigmoid(pre_act)
    return (
        cot_rows.astype(jnp.float32) * gate_value * (1.0 + pre_act * (1.0 - gate_value))
    ).astype(jnp.bfloat16)


def place_kernel(pick, valid, *refs):
    got, (out, held, zeros, in_sem, out_sem) = refs[:CHUNKS], refs[CHUNKS:]
    count = out.shape[0]
    slots = count // CHUNKS
    loads = [
        pltpu.make_async_copy(got[c], held.at[pl.ds(c * slots, slots)], in_sem.at[c])
        for c in range(CHUNKS)
    ]
    for load in loads:
        load.start()
    zeros[...] = jnp.zeros_like(zeros)
    for load in loads:
        load.wait()
    for j in range(count):

        @pl.when(valid[j] != 0)
        def _():
            pltpu.make_async_copy(held.at[pick[j]], out.at[j], out_sem).start()

        @pl.when(valid[j] == 0)
        def _():
            pltpu.make_async_copy(zeros, out.at[j], out_sem).start()

    pltpu.make_async_copy(held, out, out_sem).wait()


def place(got, pick, valid):
    slots, block = got[0].shape[0], got[0].shape[1:]
    count = slots * CHUNKS
    return pl.pallas_call(
        place_kernel,
        out_shape=jax.ShapeDtypeStruct((count,) + block, got[0].dtype),
        in_specs=[pl.BlockSpec(memory_space=pltpu.SMEM)] * 2
        + [pl.BlockSpec(memory_space=pl.ANY)] * CHUNKS,
        out_specs=pl.BlockSpec(memory_space=pl.ANY),
        scratch_shapes=[
            pltpu.VMEM((count,) + block, got[0].dtype),
            pltpu.VMEM(block, got[0].dtype),
            pltpu.SemaphoreType.DMA((CHUNKS,)),
            pltpu.SemaphoreType.DMA,
        ],
    )(pick, valid, *got)


def shards(thinker_rows, proj_weight, proj_bias, cotangent, block_owner, block_offset):
    row_count, local_width = thinker_rows.shape
    width = proj_weight.shape[1]
    tensor_count = lax.axis_size("tensor")
    dp_count = lax.axis_size("dp")
    block_total = row_count // BLOCK
    per_chunk = block_total // CHUNKS
    share = per_chunk * BLOCK // tensor_count
    t = lax.axis_index("tensor")
    owner = block_owner.reshape(per_chunk, CHUNKS)
    offset = block_offset.reshape(per_chunk, CHUNKS)
    owners = jnp.arange(dp_count, dtype=jnp.int32)
    hot = owner[:, :, None] == owners[None, None, :]
    send_offset = jnp.sum(jnp.where(hot, offset[:, :, None] + 1, 0), axis=0) - 1
    got_offset = lax.all_to_all(send_offset.T, "dp", split_axis=0, concat_axis=0, tiled=True)
    rows4 = thinker_rows.reshape(per_chunk, CHUNKS, BLOCK, local_width)
    cot4 = cotangent.reshape(per_chunk, CHUNKS, BLOCK, width)
    per_block = BLOCK // share
    xs = [rows4[:, c].reshape(per_chunk * BLOCK, local_width) for c in range(CHUNKS)]
    weight_term = jnp.zeros((local_width, width), jnp.float32)
    got = []
    slopes = []
    last = None
    for c in range(CHUNKS):
        part = jnp.dot(xs[c], proj_weight, preferred_element_type=jnp.float32).astype(jnp.bfloat16)
        summed = lax.psum_scatter(part, "tensor", scatter_dimension=0, tiled=True).astype(jnp.float32)
        if last is not None:
            summed, last = lax.optimization_barrier((summed, last))
        own_cot = lax.dynamic_slice(
            cot4, (t // per_block, c, (t % per_block) * share, 0), (1, 1, share, width)
        ).reshape(share, width)
        last = slope_of(summed, proj_bias, own_cot)
        slopes.append(lax.all_gather(last, "tensor", axis=0, tiled=True))
    for c in range(CHUNKS):
        slope_rows = slopes[c]
        if c:
            slope_rows, got[-1], weight_term = lax.optimization_barrier((slope_rows, got[-1], weight_term))
        input_grad = lax.dot_general(
            slope_rows, proj_weight, (((1,), (1,)), ((), ())), preferred_element_type=jnp.float32
        ).astype(jnp.bfloat16).reshape(per_chunk, BLOCK, local_width)
        send = jnp.zeros((dp_count, BLOCK, local_width), jnp.bfloat16)
        for k in range(per_chunk):
            send = jnp.where(hot[k, c][:, None, None], input_grad[k][None], send)
        got.append(lax.all_to_all(send, "dp", split_axis=0, concat_axis=0, tiled=True))
        weight_term = weight_term + lax.dot_general(
            xs[c], slope_rows, (((0,), (0,)), ((), ())), preferred_element_type=jnp.float32
        )
    grad_scale = float(row_count * dp_count) ** (-0.5)
    proj_grad = lax.psum_scatter(
        (weight_term * grad_scale).astype(jnp.bfloat16), "dp", scatter_dimension=0, tiled=True
    ).astype(jnp.float32)
    slots = CHUNKS * dp_count
    flat_offset = got_offset.T.reshape(slots)
    match = flat_offset[None, :] == jnp.arange(2 * block_total, dtype=jnp.int32)[:, None]
    pick = jnp.sum(jnp.where(match, jnp.arange(slots, dtype=jnp.int32)[None, :], 0), axis=1)
    valid = jnp.any(match, axis=1).astype(jnp.int32)
    placed = place(got, pick, valid)
    return (placed.reshape(2 * row_count, local_width), proj_grad)


def solution(mesh):
    return jax.shard_map(
        shards,
        mesh=mesh,
        in_specs=(P("dp", "tensor"), P("tensor", None), P(), P("dp", None), P("dp"), P("dp")),
        out_specs=(P("dp", "tensor"), P(("tensor", "dp"), None)),
        check_vma=False,
    )
```

```python
import functools

import jax
import jax.numpy as jnp
from jax import lax
from jax.experimental import pallas as pl
from jax.experimental.pallas import tpu as pltpu
from jax.sharding import PartitionSpec as P

BLOCK = 128
CH = 4
N = 4
DP = 8
TILE = 16
FEAT = 512
WIDTH = 3584
HALF = WIDTH // 2
COL = 512
ROWS = N * BLOCK
MESH = pl.DeviceIdType.MESH
BF = jnp.bfloat16
F32 = jnp.float32
STEPS = (
    ("A", 0), ("R1", 0), ("A", 1), ("R1", 1), ("R2", 0), ("A", 3), ("R1", 3), ("A", 2), ("R1", 2), ("R2", 1),
    ("R3", 0), ("R2", 2), ("R5", 0), ("R2", 3), ("R3", 2), ("R3", 1), ("R6", 0), ("R5", 2), ("R3", 3), ("G2",
    0), ("R5", 1), ("R6", 2), ("G3", 0), ("R6", 1), ("G2", 2), ("G4", 0), ("G3", 2), ("G2", 1), ("D", 0),
    ("R5", 3), ("G4", 2), ("R6", 3), ("G3", 1), ("D", 2), ("W", 0), ("G2", 3), ("G4", 1), ("G3", 3), ("D", 1),
    ("W", 1), ("G4", 3), ("W", 2), ("D", 3), ("W", 3),
)


def main_kernel(
    owner, offset, bias, x_hbm, w_hbm, cot_hbm,
    got, got_info, grad_out,
    info, xv, xt, w, s, r1, r2, r4, out5, r5, cot, acc, gin, slots, pair, y1, y2,
    load_sem, cot_sem, send_sem, recv_sem, dp_send, dp_recv, own_sem, info_send, info_recv, gw_send, gw_recv,
):
    t = lax.axis_index("tensor")
    d = lax.axis_index("dp")
    z, x = t // N, t % N
    y, core = d // 2, d % 2

    def at(zz, xx):
        return {"tensor": (zz % N) * N + xx % N}

    def hop(axis, delta):
        return at(z, x + N + delta) if axis == 0 else at(z + N + delta, x)

    def peer(k):
        return {"dp": (d + k) % DP}

    def load_x(c):
        return pltpu.make_async_copy(x_hbm.at[:, c], xv.at[c], load_sem.at[c])

    def load_w():
        return pltpu.make_async_copy(w_hbm, w, load_sem.at[CH])

    def load_cot(c, h):
        return pltpu.make_async_copy(cot_hbm.at[x, c, h, z], cot.at[c, h], cot_sem.at[c, h])

    load_x(0).start()
    load_w().start()
    for c in range(1, CH):
        load_x(c).start()
    for c in range(CH):
        for h in range(2):
            load_cot(c, h).start()

    row = lax.broadcasted_iota(jnp.int32, (8, 128), 0)
    lane = lax.broadcasted_iota(jnp.int32, (8, 128), 1)
    table = jnp.zeros((8, 128), jnp.int32)
    for b in range(N * CH):
        table = jnp.where(lane == b, jnp.where(row == 0, owner[b], offset[b]), table)
    info[...] = table

    barrier = pltpu.get_barrier_semaphore()
    for axis in range(2):
        for delta in (1, -1):
            pl.semaphore_signal(barrier, inc=1, device_id=hop(axis, delta), device_id_type=MESH)
    for k in range(1, DP):
        pl.semaphore_signal(barrier, inc=1, device_id=peer(k), device_id_type=MESH)
    pl.semaphore_wait(barrier, 4 + DP - 1)

    def rows(ref, h, f, g):
        return ref.at[f, 0, g] if h == 0 else ref.at[g, 1, f]

    def copy(c, k, src, dst, dev):
        return pltpu.make_async_remote_copy(
            src_ref=src, dst_ref=dst, send_sem=send_sem.at[c, k], recv_sem=recv_sem.at[c, k],
            device_id=dev, device_id_type=MESH,
        )

    def first(h):
        return (x, z, 0, 1) if h == 0 else (z, x, 1, 0)

    LOW, HIGH, ALL = pl.ds(0, 2), pl.ds(2, 2), pl.ds(0, 4)
    CL, CR = pl.ds(0, HALF), pl.ds(HALF, HALF)

    def rs1(c, h, e):
        i, j, a, b = first(h)
        return copy(c, 2 * h + e, rows(s.at[c], h, (i + 2) % N, (LOW, HIGH)[e]), r1.at[c, h, e], hop(a, (1, -1)[e]))

    def rs2(c, h, e):
        i, j, a, b = first(h)
        return copy(c, 4 + 2 * h + e, rows(s.at[c], h, (i + (1, 3)[e]) % N, ALL), r2.at[c, h, e], hop(a, (1, -1)[e]))

    def rs4(c, h, e):
        i, j, a, b = first(h)
        return copy(c, 8 + 2 * h + e, rows(s.at[c], h, i, (j + 2) % N).at[:, (CL, CR)[e]], r4.at[c, h, e], hop(b, (1, -1)[e]))

    def rs5(c, h, e):
        i, j, a, b = first(h)
        return copy(c, 12 + 2 * h + e, out5.at[c, h, e], r5.at[c, h, e], hop(b, (1, -1)[e]))

    def ag1(c, h, e, landing=False):
        i, j, a, b = first(h)
        part = rows(s.at[c], h, i, (j + (3, 1)[e]) % N if landing else j)
        return copy(c, 16 + 2 * h + e, part, part, hop(b, (1, -1)[e]))

    def ag2(c, h, e, landing=False):
        i, j, a, b = first(h)
        part = rows(s.at[c], h, i, (j + 2) % N if landing else (j + (3, 1)[e]) % N).at[:, (CL, CR)[e]]
        return copy(c, 20 + 2 * h + e, part, part, hop(b, (1, -1)[e]))

    def ag3(c, h, e, landing=False):
        i, j, a, b = first(h)
        part = rows(s.at[c], h, (i + (3, 1)[e]) % N if landing else i, ALL)
        return copy(c, 24 + 2 * h + e, part, part, hop(a, (1, -1)[e]))

    def ag4(c, h, e, landing=False):
        i, j, a, b = first(h)
        part = rows(s.at[c], h, (i + 2) % N if landing else (i + (3, 1)[e]) % N, (LOW, HIGH)[e])
        return copy(c, 28 + 2 * h + e, part, part, hop(a, (1, -1)[e]))

    BOTH = [(h, e) for e in range(2) for h in range(2)]

    def matmul(c):
        if c == 0:
            load_w().wait()
        load_x(c).wait()

        @pl.loop(0, WIDTH // COL)
        def _(n):
            cols = pl.ds(pl.multiple_of(n * COL, COL), COL)
            out = jnp.dot(xv[c].reshape(ROWS, FEAT), w[:, cols], preferred_element_type=F32).astype(BF)
            s[c, :, :, :, :, cols] = out.reshape(N, 2, N, TILE, COL)

    def add(dst, src):
        dst[...] = (dst[...].astype(F32) + src[...].astype(F32)).astype(BF)

    def reduce1(c):
        for h, e in BOTH:
            rs1(c, h, e).start()

    def reduce2(c):
        for h, e in BOTH:
            i, j, a, b = first(h)
            rs1(c, h, e).wait_recv()
            f = (i + (1, 3)[e]) % N

            @pl.loop(0, 2)
            def _(g):
                add(rows(s.at[c], h, f, 2 * e + g), r1.at[c, h, e, g])

            rs2(c, h, e).start()

    def reduce3(c):
        for h in range(2):
            i, j, a, b = first(h)
            for e in range(2):
                rs2(c, h, e).wait_recv()

            @pl.loop(0, N)
            def _(g):
                own = rows(s.at[c], h, i, g)
                own[...] = (
                    own[...].astype(F32) + r2[c, h, 0, g].astype(F32) + r2[c, h, 1, g].astype(F32)
                ).astype(BF)

            for e in range(2):
                rs4(c, h, e).start()

    def reduce5(c):
        for make in (rs1, rs2, rs4):
            for h, e in BOTH:
                make(c, h, e).wait_send()
        for h, e in BOTH:
            i, j, a, b = first(h)
            part = rows(s.at[c], h, i, (j + (1, 3)[e]) % N)
            mine, other = ((CL, CR), (CR, CL))[e]
            out5[c, h, e, :, other] = part[:, other]
            rs4(c, h, e).wait_recv()
            out5[c, h, e, :, mine] = (part[:, mine].astype(F32) + r4[c, h, e].astype(F32)).astype(BF)
            rs5(c, h, e).start()

    def reduce6(c):
        for h in range(2):
            i, j, a, b = first(h)
            for e in range(2):
                rs5(c, h, e).wait_recv()
            load_cot(c, h).wait()

            @pl.loop(0, WIDTH // COL)
            def _(n):
                cols = pl.ds(pl.multiple_of(n * COL, COL), COL)
                own = rows(s.at[c], h, i, j)
                total = own[:, cols].astype(F32) + r5[c, h, 0, :, cols].astype(F32) + r5[c, h, 1, :, cols].astype(F32)
                pre = total + bias[cols][None, :]
                gate = 1.0 / (1.0 + jnp.exp(-pre))
                slope = cot[c, h, :, cols].astype(F32) * gate * (1.0 + pre * (1.0 - gate))
                rows(s.at[c], h, i, j)[:, cols] = slope.astype(BF)

            for e in range(2):
                ag1(c, h, e).start()

    def gather2(c):
        for h, e in BOTH:
            ag1(c, h, e, True).wait_recv()
            ag2(c, h, e).start()

    def gather3(c):
        for h in range(2):
            for e in range(2):
                ag2(c, h, e, True).wait_recv()
            for e in range(2):
                ag3(c, h, e).start()

    def gather4(c):
        for h, e in BOTH:
            ag3(c, h, e, True).wait_recv()
            ag4(c, h, e).start()

    def slot_copy(c, k):
        return pltpu.make_async_remote_copy(
            src_ref=slots.at[c, k], dst_ref=got.at[c, d], send_sem=dp_send.at[c, k], recv_sem=dp_recv.at[c, k],
            device_id=peer(k), device_id_type=MESH,
        )

    def slot_landing(c, k):
        return pltpu.make_async_remote_copy(
            src_ref=slots.at[c, k], dst_ref=got.at[c, (d + DP - k) % DP], send_sem=dp_send.at[c, k],
            recv_sem=dp_recv.at[c, k], device_id=peer(k), device_id_type=MESH,
        )

    def own_slot(c):
        return pltpu.make_async_copy(slots.at[c, 0], got.at[c, d], own_sem.at[c])

    def sent(c):
        for make in (rs5, ag1, ag2, ag3, ag4):
            for h, e in BOTH:
                make(c, h, e).wait_send()

    def landed(c, name):
        other = ("D" if name == "W" else "W", c)
        if STEPS.index((name, c)) < STEPS.index(other):
            for h, e in BOTH:
                ag4(c, h, e, True).wait_recv()

    def data_grad(c):
        landed(c, "D")

        @pl.loop(0, 2)
        def _(n):
            half = FEAT // 2
            features = pl.ds(pl.multiple_of(n * half, half), half)
            out = lax.dot_general(
                s[c].reshape(ROWS, WIDTH), w[features, :], (((1,), (1,)), ((), ())), preferred_element_type=F32
            ).astype(BF)
            gin[:, :, features] = out.reshape(N, BLOCK, half)

        for k in range(DP):
            target = (d + k) % DP
            pick = jnp.int32(0)
            for b in range(1, N):
                pick = jnp.where(owner[b * CH + c] == target, b, pick)
            slots[c, k] = gin[pick]
            if k:
                slot_copy(c, k).start()
            else:
                own_slot(c).start()

    def weight_grad(c):
        landed(c, "W")
        place = [b for name, b in STEPS if name == "W"].index(c)
        if place == CH - 1:
            sent(0)
        xt[...] = xv[c].reshape(ROWS, FEAT).T

        @pl.loop(0, WIDTH // COL)
        def _(n):
            cols = pl.ds(pl.multiple_of(n * COL, COL), COL)
            part = s[c, :, :, :, :, cols].reshape(ROWS, COL)
            out = jnp.dot(xt[...], part, preferred_element_type=F32)
            if place == 0:
                acc[:, cols] = out
            elif place < CH - 1:
                acc[:, cols] += out
            else:
                full = ((acc[:, cols] + out) * (float(ROWS * CH * DP) ** -0.5)).astype(BF)
                s[0, :, :, :, :, cols] = full.reshape(N, 2, N, TILE, COL)

    def info_copy(k):
        return pltpu.make_async_remote_copy(
            src_ref=info, dst_ref=got_info.at[d], send_sem=info_send.at[k], recv_sem=info_recv.at[k],
            device_id=peer(k), device_id_type=MESH,
        )

    def info_landing(k):
        return pltpu.make_async_remote_copy(
            src_ref=info, dst_ref=got_info.at[(d + DP - k) % DP], send_sem=info_send.at[k], recv_sem=info_recv.at[k],
            device_id=peer(k), device_id_type=MESH,
        )

    own_info = pltpu.make_async_copy(info, got_info.at[d], info_send.at[0])
    own_info.start()
    for k in range(1, DP):
        info_copy(k).start()

    phases = {
        "A": matmul, "R1": reduce1, "R2": reduce2, "R3": reduce3, "R5": reduce5, "R6": reduce6,
        "G2": gather2, "G3": gather3, "G4": gather4, "D": data_grad, "W": weight_grad,
    }
    for name, c in STEPS:
        phases[name](c)

    def gw(k, src, dst, dev):
        return pltpu.make_async_remote_copy(
            src_ref=src, dst_ref=dst, send_sem=gw_send.at[k], recv_sem=gw_recv.at[k],
            device_id=dev, device_id_type=MESH,
        )

    sibling = {"dp": 2 * y + 1 - core}
    ring = [{"dp": (d + 2) % DP}, {"dp": (d + DP - 2) % DP}]
    swap = gw(0, s.at[0, :, 1 - core], pair, sibling)
    swap.start()
    swap.wait_recv()

    @pl.loop(0, N)
    def _(k):
        @pl.loop(0, N)
        def _(g):
            add(s.at[0, k, core, g], pair.at[k, g])

    step1 = [gw(1 + e, s.at[0, (y + 2) % N, core, (LOW, HIGH)[e]], y1.at[e], ring[e]) for e in range(2)]
    step2 = [gw(3 + e, s.at[0, (y + (1, 3)[e]) % N, core], y2.at[e], ring[e]) for e in range(2)]
    for e in range(2):
        step1[e].start()
    for e in range(2):
        step1[e].wait_recv()

        @pl.loop(0, 2)
        def _(g):
            add(s.at[0, (y + (1, 3)[e]) % N, core, 2 * e + g], y1.at[e, g])

        step2[e].start()
    for e in range(2):
        step2[e].wait_recv()

    @pl.loop(0, N)
    def _(g):
        grad_out[g] = s[0, y, core, g].astype(F32) + y2[0, g].astype(F32) + y2[1, g].astype(F32)

    swap.wait_send()
    for e in range(2):
        step1[e].wait_send()
        step2[e].wait_send()
    own_info.wait()
    for k in range(1, DP):
        info_copy(k).wait_send()
        info_landing(k).wait_recv()
    for c in range(CH):
        if c:
            sent(c)
        own_slot(c).wait()
        for k in range(1, DP):
            slot_copy(c, k).wait_send()
            slot_landing(c, k).wait_recv()


def place_kernel(me, info, got, grad, out, grad_out, table, held, zeros, passed, flag, info_sem, in_sem, grad_sem, out_sem):
    fetch = pltpu.make_async_copy(info, table, info_sem)
    fetch.start()
    load = pltpu.make_async_copy(got, held, in_sem)
    load.start()
    take = pltpu.make_async_copy(grad, passed, grad_sem)
    take.start()
    zeros[...] = jnp.zeros_like(zeros)
    count = out.shape[0]
    for j in range(count):
        flag[j] = 0
    fetch.wait()
    load.wait()
    take.wait()
    give = pltpu.make_async_copy(passed, grad_out, grad_sem)
    give.start()
    mine = me[0]
    for source in range(DP):
        for b in range(N):
            for c in range(CH):

                @pl.when(table[source, 0, b * CH + c] == mine)
                def _():
                    row = table[source, 1, b * CH + c]
                    flag[row] = 1
                    pltpu.make_async_copy(held.at[c, source], out.at[row], out_sem).start()

    for j in range(count):

        @pl.when(flag[j] == 0)
        def _():
            pltpu.make_async_copy(zeros, out.at[j], out_sem).start()

    pltpu.make_async_copy(out, out, out_sem).wait()
    give.wait()


def shards(thinker_rows, proj_weight, proj_bias, cotangent, block_owner, block_offset):
    vmem = pl.BlockSpec(memory_space=pltpu.VMEM)
    smem = pl.BlockSpec(memory_space=pltpu.SMEM)
    hbm = pl.BlockSpec(memory_space=pl.ANY)
    tile = (TILE, WIDTH)
    dma = pltpu.SemaphoreType.DMA
    got, got_info, grad = pl.pallas_call(
        main_kernel,
        out_shape=(
            jax.ShapeDtypeStruct((CH, DP, BLOCK, FEAT), BF),
            jax.ShapeDtypeStruct((DP, 8, 128), jnp.int32),
            jax.ShapeDtypeStruct((N,) + tile, F32),
        ),
        in_specs=[smem, smem, vmem, hbm, hbm, hbm],
        out_specs=(hbm, hbm, vmem),
        scratch_shapes=[
            pltpu.VMEM((8, 128), jnp.int32),
            pltpu.VMEM((CH, N, BLOCK, FEAT), BF),
            pltpu.VMEM((FEAT, ROWS), BF),
            pltpu.VMEM((FEAT, WIDTH), BF),
            pltpu.VMEM((CH, N, 2, N) + tile, BF),
            pltpu.VMEM((CH, 2, 2, 2) + tile, BF),
            pltpu.VMEM((CH, 2, 2, N) + tile, BF),
            pltpu.VMEM((CH, 2, 2, TILE, HALF), BF),
            pltpu.VMEM((CH, 2, 2) + tile, BF),
            pltpu.VMEM((CH, 2, 2) + tile, BF),
            pltpu.VMEM((CH, 2) + tile, BF),
            pltpu.VMEM((FEAT, WIDTH), F32),
            pltpu.VMEM((N, BLOCK, FEAT), BF),
            pltpu.VMEM((CH, DP, BLOCK, FEAT), BF),
            pltpu.VMEM((N, N) + tile, BF),
            pltpu.VMEM((2, 2) + tile, BF),
            pltpu.VMEM((2, N) + tile, BF),
            dma((CH + 1,)),
            dma((CH, 2)),
            dma((CH, 32)),
            dma((CH, 32)),
            dma((CH, DP)),
            dma((CH, DP)),
            dma((CH,)),
            dma((DP,)),
            dma((DP,)),
            dma((5,)),
            dma((5,)),
        ],
        compiler_params=pltpu.CompilerParams(
            collective_id=0, has_side_effects=True, vmem_limit_bytes=67_000_000
        ),
        name="fused_backward",
    )(
        block_owner,
        block_offset,
        proj_bias,
        thinker_rows.reshape(N, CH, BLOCK, FEAT),
        proj_weight,
        cotangent.reshape(N, CH, 2, N, TILE, WIDTH),
    )
    placed, grad = pl.pallas_call(
        place_kernel,
        out_shape=(
            jax.ShapeDtypeStruct((CH * DP, BLOCK, FEAT), BF),
            jax.ShapeDtypeStruct((N,) + tile, F32),
        ),
        in_specs=[smem, hbm, hbm, hbm],
        out_specs=(hbm, hbm),
        scratch_shapes=[
            pltpu.SMEM((DP, 8, 128), jnp.int32),
            pltpu.VMEM((CH, DP, BLOCK, FEAT), BF),
            pltpu.VMEM((BLOCK, FEAT), BF),
            pltpu.VMEM((N,) + tile, F32),
            pltpu.SMEM((CH * DP,), jnp.int32),
            dma,
            dma,
            dma,
            dma,
        ],
        name="place_blocks",
    )(lax.axis_index("dp").reshape(1), got_info, got, grad)
    return (placed.reshape(CH * DP * BLOCK, FEAT), grad.reshape(N * TILE, WIDTH))


def solution(mesh):
    return jax.shard_map(
        shards,
        mesh=mesh,
        in_specs=(P("dp", "tensor"), P("tensor", None), P(), P("dp", None), P("dp"), P("dp")),
        out_specs=(P("dp", "tensor"), P(("tensor", "dp"), None)),
        check_vma=False,
    )
```

```python
import functools

import jax
import jax.numpy as jnp
from jax import lax
from jax.experimental import pallas as pl
from jax.experimental.pallas import tpu as pltpu
from jax.sharding import PartitionSpec as P

BLOCK = 128
CH = 4
PARTS = 2
ALL_CH = CH * PARTS
N = 4
DP = 8
TILE = 16
FEAT = 512
WIDTH = 3584
PART = WIDTH // PARTS
HALF = PART // 2
COL = 256
ROWS = N * BLOCK
MESH = pl.DeviceIdType.MESH
BF = jnp.bfloat16
F32 = jnp.float32
STEPS = (
    ("A", 1), ("R1", 1), ("A", 0), ("R1", 0), ("A", 3), ("R1", 3), ("A", 5), ("R1", 5), ("R2", 0), ("A", 6),
    ("R2", 3), ("R3", 0), ("R2", 1), ("A", 2), ("A", 4), ("R5", 0), ("R1", 2), ("R1", 6), ("R3", 3), ("R2", 5),
    ("R3", 1), ("R5", 3), ("R6", 0), ("R1", 4), ("R2", 2), ("R5", 1), ("R2", 4), ("A", 7), ("R3", 2), ("R6", 3),
    ("R2", 6), ("G2", 3), ("R3", 4), ("R5", 2), ("R6", 1), ("G2", 0), ("G3", 3), ("G2", 1), ("G3", 0),
    ("R5", 4), ("R6", 2), ("G4", 0), ("G3", 1), ("R6", 4), ("R3", 6), ("G2", 2), ("R3", 5), ("G4", 3),
    ("G2", 4), ("R5", 6), ("R5", 5), ("R1", 7), ("G3", 2), ("R6", 5), ("W", 0), ("DL", 3), ("G4", 1), ("W", 3),
    ("G4", 2), ("G3", 4), ("W", 1), ("G2", 5), ("R2", 7), ("W", 2), ("Y1", 0), ("G4", 4), ("R6", 6), ("R3", 7),
    ("G3", 5), ("Y2", 0), ("D", 0), ("R5", 7), ("G2", 6), ("G4", 5), ("R6", 7), ("G3", 6), ("D", 1), ("Y3", 0),
    ("G2", 7), ("G4", 6), ("W", 5), ("G3", 7), ("D", 2), ("G4", 7), ("W", 6), ("W", 4), ("W", 7), ("D", 3),
    ("Y1", 1), ("Y2", 1), ("Y3", 1),
)


def main_kernel(
    owner, offset, bias, x_hbm, w_hbm, cot_hbm,
    got, got_info, grad_out,
    info, xv, xt, w, s, r1, r2, r4, out5, r5, cot, acc, left, gin, slots, stage, pair, y1, y2,
    load_sem, cot_sem, send_sem, recv_sem, dp_send, dp_recv, own_sem, info_send, info_recv, gw_send, gw_recv,
):
    t = lax.axis_index("tensor")
    d = lax.axis_index("dp")
    z, x = t // N, t % N
    y, core = d // 2, d % 2

    def at(zz, xx):
        return {"tensor": (zz % N) * N + xx % N}

    def hop(axis, delta):
        return at(z, x + N + delta) if axis == 0 else at(z + N + delta, x)

    def peer(k):
        return {"dp": (d + k) % DP}

    def load_x(c):
        return pltpu.make_async_copy(x_hbm.at[:, c], xv.at[c], load_sem.at[c])

    def load_w(part):
        cols = pl.ds(part * PART, PART)
        return pltpu.make_async_copy(w_hbm.at[:, cols], w.at[:, cols], load_sem.at[CH + part])

    def load_cot(c, h):
        src = cot_hbm.at[x, c % CH, h, z].at[:, pl.ds(c // CH * PART, PART)]
        return pltpu.make_async_copy(src, cot.at[c, h], cot_sem.at[c, h])

    arrivals = []
    for name, c in STEPS:
        if name == "A" and c % CH not in arrivals:
            arrivals.append(c % CH)
    load_x(arrivals[0]).start()
    load_w(0).start()
    for c in arrivals[1:]:
        load_x(c).start()
    load_w(1).start()
    for c in range(ALL_CH):
        for h in range(2):
            load_cot(c, h).start()

    row = lax.broadcasted_iota(jnp.int32, (8, 128), 0)
    lane = lax.broadcasted_iota(jnp.int32, (8, 128), 1)
    table = jnp.zeros((8, 128), jnp.int32)
    for b in range(N * CH):
        table = jnp.where(lane == b, jnp.where(row == 0, owner[b], offset[b]), table)
    info[...] = table

    barrier = pltpu.get_barrier_semaphore()
    for axis in range(2):
        for delta in (1, -1):
            pl.semaphore_signal(barrier, inc=1, device_id=hop(axis, delta), device_id_type=MESH)
    for k in range(1, DP):
        pl.semaphore_signal(barrier, inc=1, device_id=peer(k), device_id_type=MESH)
    pl.semaphore_wait(barrier, 4 + DP - 1)

    def rows(ref, h, f, g):
        return ref.at[f, 0, g] if h == 0 else ref.at[g, 1, f]

    def copy(c, k, src, dst, dev):
        return pltpu.make_async_remote_copy(
            src_ref=src, dst_ref=dst, send_sem=send_sem.at[c, k], recv_sem=recv_sem.at[c, k],
            device_id=dev, device_id_type=MESH,
        )

    def first(h):
        return (x, z, 0, 1) if h == 0 else (z, x, 1, 0)

    LOW, HIGH, ALL = pl.ds(0, 2), pl.ds(2, 2), pl.ds(0, 4)
    CL, CR = pl.ds(0, HALF), pl.ds(HALF, HALF)

    def rs1(c, h, e):
        i, j, a, b = first(h)
        return copy(c, 2 * h + e, rows(s.at[c], h, (i + 2) % N, (LOW, HIGH)[e]), r1.at[c, h, e], hop(a, (1, -1)[e]))

    def rs2(c, h, e):
        i, j, a, b = first(h)
        return copy(c, 4 + 2 * h + e, rows(s.at[c], h, (i + (1, 3)[e]) % N, ALL), r2.at[c, h, e], hop(a, (1, -1)[e]))

    def rs4(c, h, e):
        i, j, a, b = first(h)
        return copy(c, 8 + 2 * h + e, rows(s.at[c], h, i, (j + 2) % N).at[:, (CL, CR)[e]], r4.at[c, h, e], hop(b, (1, -1)[e]))

    def rs5(c, h, e):
        i, j, a, b = first(h)
        return copy(c, 12 + 2 * h + e, out5.at[c, h, e], r5.at[c, h, e], hop(b, (1, -1)[e]))

    def ag1(c, h, e, landing=False):
        i, j, a, b = first(h)
        part = rows(s.at[c], h, i, (j + (3, 1)[e]) % N if landing else j)
        return copy(c, 16 + 2 * h + e, part, part, hop(b, (1, -1)[e]))

    def ag2(c, h, e, landing=False):
        i, j, a, b = first(h)
        part = rows(s.at[c], h, i, (j + 2) % N if landing else (j + (3, 1)[e]) % N).at[:, (CL, CR)[e]]
        return copy(c, 20 + 2 * h + e, part, part, hop(b, (1, -1)[e]))

    def ag3(c, h, e, landing=False):
        i, j, a, b = first(h)
        part = rows(s.at[c], h, (i + (3, 1)[e]) % N if landing else i, ALL)
        return copy(c, 24 + 2 * h + e, part, part, hop(a, (1, -1)[e]))

    def ag4(c, h, e, landing=False):
        i, j, a, b = first(h)
        part = rows(s.at[c], h, (i + 2) % N if landing else (i + (3, 1)[e]) % N, (LOW, HIGH)[e])
        return copy(c, 28 + 2 * h + e, part, part, hop(a, (1, -1)[e]))

    BOTH = [(h, e) for e in range(2) for h in range(2)]

    def tile(base, n):
        return pl.ds(pl.multiple_of(base + n * COL, COL), COL)

    def matmul(c):
        rc, base = c % CH, c // CH * PART
        if base not in loaded:
            loaded.add(base)
            load_w(c // CH).wait()
        if ("x", rc) not in loaded:
            loaded.add(("x", rc))
            load_x(rc).wait()

        @pl.loop(0, PART // COL)
        def _(n):
            out = jnp.dot(xv[rc].reshape(ROWS, FEAT), w[:, tile(base, n)], preferred_element_type=F32).astype(BF)
            s[c, :, :, :, :, tile(0, n)] = out.reshape(N, 2, N, TILE, COL)

    def add(dst, src):
        dst[...] = (dst[...].astype(F32) + src[...].astype(F32)).astype(BF)

    def reduce1(c):
        for h, e in BOTH:
            rs1(c, h, e).start()

    def reduce2(c):
        for h, e in BOTH:
            i, j, a, b = first(h)
            rs1(c, h, e).wait_recv()
            f = (i + (1, 3)[e]) % N

            @pl.loop(0, 2)
            def _(g):
                add(rows(s.at[c], h, f, 2 * e + g), r1.at[c, h, e, g])

            rs2(c, h, e).start()

    def reduce3(c):
        for h in range(2):
            i, j, a, b = first(h)
            for e in range(2):
                rs2(c, h, e).wait_recv()

            @pl.loop(0, N)
            def _(g):
                own = rows(s.at[c], h, i, g)
                own[...] = (
                    own[...].astype(F32) + r2[c, h, 0, g].astype(F32) + r2[c, h, 1, g].astype(F32)
                ).astype(BF)

            for e in range(2):
                rs4(c, h, e).start()

    def reduce5(c):
        for make in (rs1, rs2, rs4):
            for h, e in BOTH:
                make(c, h, e).wait_send()
        for h, e in BOTH:
            i, j, a, b = first(h)
            part = rows(s.at[c], h, i, (j + (1, 3)[e]) % N)
            mine, other = ((CL, CR), (CR, CL))[e]
            out5[c, h, e, :, other] = part[:, other]
            rs4(c, h, e).wait_recv()
            out5[c, h, e, :, mine] = (part[:, mine].astype(F32) + r4[c, h, e].astype(F32)).astype(BF)
            rs5(c, h, e).start()

    def reduce6(c):
        for h in range(2):
            i, j, a, b = first(h)
            for e in range(2):
                rs5(c, h, e).wait_recv()
            load_cot(c, h).wait()

            @pl.loop(0, PART // COL)
            def _(n):
                cols = tile(0, n)
                own = rows(s.at[c], h, i, j)
                total = own[:, cols].astype(F32) + r5[c, h, 0, :, cols].astype(F32) + r5[c, h, 1, :, cols].astype(F32)
                pre = total + bias[tile(c // CH * PART, n)][None, :]
                gate = 1.0 / (1.0 + jnp.exp(-pre))
                slope = cot[c, h, :, cols].astype(F32) * gate * (1.0 + pre * (1.0 - gate))
                rows(s.at[c], h, i, j)[:, cols] = slope.astype(BF)

            for e in range(2):
                ag1(c, h, e).start()

    def gather2(c):
        for h, e in BOTH:
            ag1(c, h, e, True).wait_recv()
            ag2(c, h, e).start()

    def gather3(c):
        for h in range(2):
            for e in range(2):
                ag2(c, h, e, True).wait_recv()
            for e in range(2):
                ag3(c, h, e).start()

    def gather4(c):
        for h, e in BOTH:
            ag3(c, h, e, True).wait_recv()
            ag4(c, h, e).start()

    def slot_copy(c, k):
        return pltpu.make_async_remote_copy(
            src_ref=slots.at[c, k], dst_ref=got.at[c, d], send_sem=dp_send.at[c, k], recv_sem=dp_recv.at[c, k],
            device_id=peer(k), device_id_type=MESH,
        )

    def slot_landing(c, k):
        return pltpu.make_async_remote_copy(
            src_ref=slots.at[c, k], dst_ref=got.at[c, (d + DP - k) % DP], send_sem=dp_send.at[c, k],
            recv_sem=dp_recv.at[c, k], device_id=peer(k), device_id_type=MESH,
        )

    def own_slot(c):
        return pltpu.make_async_copy(slots.at[c, 0], got.at[c, d], own_sem.at[c])

    def sent(c):
        for make in (rs5, ag1, ag2, ag3, ag4):
            for h, e in BOTH:
                make(c, h, e).wait_send()

    def landed(c):
        if c not in seen:
            seen.add(c)
            for h, e in BOTH:
                ag4(c, h, e, True).wait_recv()

    def feature_tile(n):
        half = FEAT // 2
        return pl.ds(pl.multiple_of(n * half, half), half)

    def grad_part(c, n):
        cols = pl.ds(c // CH * PART, PART)
        return lax.dot_general(
            s[c].reshape(ROWS, PART), w[feature_tile(n), cols], (((1,), (1,)), ((), ())), preferred_element_type=F32
        )

    def data_grad_left(c):
        landed(c)

        @pl.loop(0, 2)
        def _(n):
            left[:, feature_tile(n)] = grad_part(c, n)

    def data_grad(c):
        landed(c)
        landed(c + CH)

        @pl.loop(0, 2)
        def _(n):
            if ("DL", c) in STEPS:
                out = left[:, feature_tile(n)]
            else:
                out = grad_part(c, n)
            out = (out + grad_part(c + CH, n)).astype(BF)
            gin[:, :, feature_tile(n)] = out.reshape(N, BLOCK, FEAT // 2)

        for k in range(DP):
            target = (d + k) % DP
            pick = jnp.int32(0)
            for b in range(1, N):
                pick = jnp.where(owner[b * CH + c] == target, b, pick)
            slots[c, k] = gin[pick]
            if k:
                slot_copy(c, k).start()
            else:
                own_slot(c).start()

    def weight_grad(c):
        landed(c)
        rc, part = c % CH, c // CH
        place = [b for name, b in STEPS if name == "W" and b // CH == part].index(c)
        if rc not in turned:
            turned.add(rc)
            xt[rc] = xv[rc].reshape(ROWS, FEAT).T

        @pl.loop(0, PART // COL)
        def _(n):
            rows_here = s[c, :, :, :, :, tile(0, n)].reshape(ROWS, COL)
            out = jnp.dot(xt[rc], rows_here, preferred_element_type=F32)
            cols = tile(part * PART, n)
            if place == 0:
                acc[:, cols] = out
            elif place < CH - 1:
                acc[:, cols] += out
            else:
                full = ((acc[:, cols] + out) * (float(ROWS * CH * DP) ** -0.5)).astype(BF)
                stage[:, :, :, :, tile(0, n)] = full.reshape(N, 2, N, TILE, COL)

        if place == CH - 1:
            swap(part).start()

    def gw(part, k, src, dst, dev):
        return pltpu.make_async_remote_copy(
            src_ref=src, dst_ref=dst, send_sem=gw_send.at[part, k], recv_sem=gw_recv.at[part, k],
            device_id=dev, device_id_type=MESH,
        )

    def swap(part):
        return gw(part, 0, stage.at[:, 1 - core], pair.at[part], {"dp": 2 * y + 1 - core})

    def ring(e):
        return {"dp": (d + (2, DP - 2)[e]) % DP}

    def ring1(part, e):
        return gw(part, 1 + e, stage.at[(y + 2) % N, core, (LOW, HIGH)[e]], y1.at[part, e], ring(e))

    def ring2(part, e):
        return gw(part, 3 + e, stage.at[(y + (1, 3)[e]) % N, core], y2.at[part, e], ring(e))

    def dp_reduce1(part):
        swap(part).wait_recv()

        @pl.loop(0, N)
        def _(k):
            @pl.loop(0, N)
            def _(g):
                add(stage.at[k, core, g], pair.at[part, k, g])

        for e in range(2):
            ring1(part, e).start()

    def dp_reduce2(part):
        for e in range(2):
            ring1(part, e).wait_recv()

            @pl.loop(0, 2)
            def _(g):
                add(stage.at[(y + (1, 3)[e]) % N, core, 2 * e + g], y1.at[part, e, g])

            ring2(part, e).start()

    def dp_reduce3(part):
        for e in range(2):
            ring2(part, e).wait_recv()

        @pl.loop(0, N)
        def _(g):
            grad_out[g, :, pl.ds(part * PART, PART)] = (
                stage[y, core, g].astype(F32) + y2[part, 0, g].astype(F32) + y2[part, 1, g].astype(F32)
            )

        swap(part).wait_send()
        for e in range(2):
            ring1(part, e).wait_send()
            ring2(part, e).wait_send()

    def info_copy(k):
        return pltpu.make_async_remote_copy(
            src_ref=info, dst_ref=got_info.at[d], send_sem=info_send.at[k], recv_sem=info_recv.at[k],
            device_id=peer(k), device_id_type=MESH,
        )

    def info_landing(k):
        return pltpu.make_async_remote_copy(
            src_ref=info, dst_ref=got_info.at[(d + DP - k) % DP], send_sem=info_send.at[k], recv_sem=info_recv.at[k],
            device_id=peer(k), device_id_type=MESH,
        )

    own_info = pltpu.make_async_copy(info, got_info.at[d], info_send.at[0])
    own_info.start()
    for k in range(1, DP):
        info_copy(k).start()

    phases = {
        "A": matmul, "R1": reduce1, "R2": reduce2, "R3": reduce3, "R5": reduce5, "R6": reduce6,
        "G2": gather2, "G3": gather3, "G4": gather4, "DL": data_grad_left, "D": data_grad,
        "W": weight_grad, "Y1": dp_reduce1, "Y2": dp_reduce2, "Y3": dp_reduce3,
    }
    seen, turned, loaded = set(), set(), set()
    for name, c in STEPS:
        phases[name](c)

    own_info.wait()
    for k in range(1, DP):
        info_copy(k).wait_send()
        info_landing(k).wait_recv()
    for c in range(ALL_CH):
        sent(c)
    for c in range(CH):
        own_slot(c).wait()
        for k in range(1, DP):
            slot_copy(c, k).wait_send()
            slot_landing(c, k).wait_recv()


def place_kernel(me, info, got, grad, out, grad_out, table, held, zeros, passed, flag, info_sem, in_sem, grad_sem, out_sem):
    fetch = pltpu.make_async_copy(info, table, info_sem)
    fetch.start()
    load = pltpu.make_async_copy(got, held, in_sem)
    load.start()
    take = pltpu.make_async_copy(grad, passed, grad_sem)
    take.start()
    zeros[...] = jnp.zeros_like(zeros)
    count = out.shape[0]
    for j in range(count):
        flag[j] = 0
    fetch.wait()
    load.wait()
    take.wait()
    give = pltpu.make_async_copy(passed, grad_out, grad_sem)
    give.start()
    mine = me[0]
    for source in range(DP):
        for b in range(N):
            for c in range(CH):

                @pl.when(table[source, 0, b * CH + c] == mine)
                def _():
                    row = table[source, 1, b * CH + c]
                    flag[row] = 1
                    pltpu.make_async_copy(held.at[c, source], out.at[row], out_sem).start()

    for j in range(count):

        @pl.when(flag[j] == 0)
        def _():
            pltpu.make_async_copy(zeros, out.at[j], out_sem).start()

    pltpu.make_async_copy(out, out, out_sem).wait()
    give.wait()


def shards(thinker_rows, proj_weight, proj_bias, cotangent, block_owner, block_offset):
    vmem = pl.BlockSpec(memory_space=pltpu.VMEM)
    smem = pl.BlockSpec(memory_space=pltpu.SMEM)
    hbm = pl.BlockSpec(memory_space=pl.ANY)
    tile = (TILE, PART)
    row = (TILE, WIDTH)
    dma = pltpu.SemaphoreType.DMA
    got, got_info, grad = pl.pallas_call(
        main_kernel,
        out_shape=(
            jax.ShapeDtypeStruct((CH, DP, BLOCK, FEAT), BF),
            jax.ShapeDtypeStruct((DP, 8, 128), jnp.int32),
            jax.ShapeDtypeStruct((N,) + row, F32),
        ),
        in_specs=[smem, smem, vmem, hbm, hbm, hbm],
        out_specs=(hbm, hbm, vmem),
        scratch_shapes=[
            pltpu.VMEM((8, 128), jnp.int32),
            pltpu.VMEM((CH, N, BLOCK, FEAT), BF),
            pltpu.VMEM((CH, FEAT, ROWS), BF),
            pltpu.VMEM((FEAT, WIDTH), BF),
            pltpu.VMEM((ALL_CH, N, 2, N) + tile, BF),
            pltpu.VMEM((ALL_CH, 2, 2, 2) + tile, BF),
            pltpu.VMEM((ALL_CH, 2, 2, N) + tile, BF),
            pltpu.VMEM((ALL_CH, 2, 2, TILE, HALF), BF),
            pltpu.VMEM((ALL_CH, 2, 2) + tile, BF),
            pltpu.VMEM((ALL_CH, 2, 2) + tile, BF),
            pltpu.VMEM((ALL_CH, 2) + tile, BF),
            pltpu.VMEM((FEAT, WIDTH), F32),
            pltpu.VMEM((ROWS, FEAT), F32),
            pltpu.VMEM((N, BLOCK, FEAT), BF),
            pltpu.VMEM((CH, DP, BLOCK, FEAT), BF),
            pltpu.VMEM((N, 2, N) + tile, BF),
            pltpu.VMEM((PARTS, N, N) + tile, BF),
            pltpu.VMEM((PARTS, 2, 2) + tile, BF),
            pltpu.VMEM((PARTS, 2, N) + tile, BF),
            dma((CH + PARTS,)),
            dma((ALL_CH, 2)),
            dma((ALL_CH, 32)),
            dma((ALL_CH, 32)),
            dma((CH, DP)),
            dma((CH, DP)),
            dma((CH,)),
            dma((DP,)),
            dma((DP,)),
            dma((PARTS, 5)),
            dma((PARTS, 5)),
        ],
        compiler_params=pltpu.CompilerParams(
            collective_id=0, has_side_effects=True, vmem_limit_bytes=67_000_000
        ),
        name="fused_backward",
    )(
        block_owner,
        block_offset,
        proj_bias,
        thinker_rows.reshape(N, CH, BLOCK, FEAT),
        proj_weight,
        cotangent.reshape(N, CH, 2, N, TILE, WIDTH),
    )
    placed, grad = pl.pallas_call(
        place_kernel,
        out_shape=(
            jax.ShapeDtypeStruct((CH * DP, BLOCK, FEAT), BF),
            jax.ShapeDtypeStruct((N,) + row, F32),
        ),
        in_specs=[smem, hbm, hbm, hbm],
        out_specs=(hbm, hbm),
        scratch_shapes=[
            pltpu.SMEM((DP, 8, 128), jnp.int32),
            pltpu.VMEM((CH, DP, BLOCK, FEAT), BF),
            pltpu.VMEM((BLOCK, FEAT), BF),
            pltpu.VMEM((N,) + row, F32),
            pltpu.SMEM((CH * DP,), jnp.int32),
            dma,
            dma,
            dma,
            dma,
        ],
        name="place_blocks",
    )(lax.axis_index("dp").reshape(1), got_info, got, grad)
    return (placed.reshape(CH * DP * BLOCK, FEAT), grad.reshape(N * TILE, WIDTH))


def solution(mesh):
    return jax.shard_map(
        shards,
        mesh=mesh,
        in_specs=(P("dp", "tensor"), P("tensor", None), P(), P("dp", None), P("dp"), P("dp")),
        out_specs=(P("dp", "tensor"), P(("tensor", "dp"), None)),
        check_vma=False,
    )
```

```python
import functools

import jax
import jax.numpy as jnp
from jax import lax
from jax.experimental import pallas as pl
from jax.experimental.pallas import tpu as pltpu
from jax.sharding import PartitionSpec as P

BLOCK = 128
CH = 4
PARTS = 2
ALL_CH = CH * PARTS
N = 4
DP = 8
TILE = 16
FEAT = 512
WIDTH = 3584
PART = WIDTH // PARTS
HALF = PART // 2
COL = 256
ROWS = N * BLOCK
FIRST, REST = (4, 2, 6), (3, 5, 7, 1, 0)
MESH = pl.DeviceIdType.MESH
BF = jnp.bfloat16
F32 = jnp.float32
STEPS = (
    ("A", 1), ("R1", 1), ("A", 5), ("R1", 5), ("A", 4), ("R1", 4), ("R2", 1), ("A", 7), ("A", 6), ("A", 3),
    ("R2", 4), ("R3", 1), ("R1", 7), ("A", 0), ("R1", 0), ("R1", 3), ("A", 2), ("R2", 5), ("R2", 3), ("R5", 1),
    ("R3", 4), ("R3", 5), ("R1", 2), ("R1", 6), ("R6", 1), ("R2", 2), ("R5", 5), ("R2", 7), ("R3", 2),
    ("R2", 0), ("R5", 2), ("R6", 5), ("R5", 4), ("G2", 1), ("R3", 0), ("R3", 3), ("G2", 5), ("R2", 6),
    ("R5", 0), ("R6", 4), ("R5", 3), ("R6", 2), ("G3", 1), ("G2", 4), ("G3", 5), ("R6", 0), ("R3", 6),
    ("G4", 1), ("R5", 6), ("G2", 0), ("G4", 5), ("G2", 2), ("G3", 4), ("G3", 0), ("R6", 3), ("D", 1), ("E", 1),
    ("W", 5), ("G4", 4), ("G2", 3), ("R6", 6), ("G4", 0), ("W", 1), ("G3", 2), ("G3", 3), ("R3", 7), ("G4", 2),
    ("G2", 6), ("D", 0), ("E", 0), ("G4", 3), ("W", 0), ("R5", 7), ("W", 2), ("G3", 6), ("W", 3), ("R6", 7),
    ("Y1", 0), ("G4", 6), ("G2", 7), ("Y2", 0), ("G3", 7), ("D", 2), ("DL", 3), ("G4", 7), ("E", 2), ("W", 4),
    ("W", 6), ("D", 3), ("Y3", 0), ("W", 7), ("Y1", 1), ("E", 3), ("Y2", 1), ("Y3", 1),
)


def main_kernel(
    owner, offset, bias, x_hbm, w_hbm, cot_hbm,
    got, got_info, grad_out,
    info, xv, xt, w, s, r1, r2, r4, out5, r5, cot, acc, left, gin, slots, stage, pair, y1, y2,
    load_sem, cot_sem, send_sem, recv_sem, dp_send, dp_recv, own_sem, info_send, info_recv, gw_send, gw_recv,
):
    t = lax.axis_index("tensor")
    d = lax.axis_index("dp")
    z, x = t // N, t % N
    y, core = d // 2, d % 2

    def at(zz, xx):
        return {"tensor": (zz % N) * N + xx % N}

    def hop(axis, delta):
        return at(z, x + N + delta) if axis == 0 else at(z + N + delta, x)

    def peer(k):
        return {"dp": (d + k) % DP}

    def load_x(c):
        return pltpu.make_async_copy(x_hbm.at[:, c], xv.at[c], load_sem.at[c])

    def load_w(part):
        cols = pl.ds(part * PART, PART)
        return pltpu.make_async_copy(w_hbm.at[:, cols], w.at[:, cols], load_sem.at[CH + part])

    def load_cot(c, h):
        src = cot_hbm.at[x, c % CH, h, z].at[:, pl.ds(c // CH * PART, PART)]
        return pltpu.make_async_copy(src, cot.at[c, h], cot_sem.at[c, h])

    arrivals = []
    for name, c in STEPS:
        if name == "A" and c % CH not in arrivals:
            arrivals.append(c % CH)
    load_x(arrivals[0]).start()
    load_w(0).start()
    for c in arrivals[1:]:
        load_x(c).start()
    load_w(1).start()
    for c in range(ALL_CH):
        for h in range(2):
            load_cot(c, h).start()

    row = lax.broadcasted_iota(jnp.int32, (8, 128), 0)
    lane = lax.broadcasted_iota(jnp.int32, (8, 128), 1)
    table = jnp.zeros((8, 128), jnp.int32)
    for b in range(N * CH):
        table = jnp.where(lane == b, jnp.where(row == 0, owner[b], offset[b]), table)
    info[...] = table

    barrier = pltpu.get_barrier_semaphore()
    for axis in range(2):
        for delta in (1, -1):
            pl.semaphore_signal(barrier, inc=1, device_id=hop(axis, delta), device_id_type=MESH)
    for k in range(1, DP):
        pl.semaphore_signal(barrier, inc=1, device_id=peer(k), device_id_type=MESH)

    def rows(ref, h, f, g):
        return ref.at[f, 0, g] if h == 0 else ref.at[g, 1, f]

    def copy(c, k, src, dst, dev):
        return pltpu.make_async_remote_copy(
            src_ref=src, dst_ref=dst, send_sem=send_sem.at[c, k], recv_sem=recv_sem.at[c, k],
            device_id=dev, device_id_type=MESH,
        )

    def first(h):
        return (x, z, 0, 1) if h == 0 else (z, x, 1, 0)

    LOW, HIGH, ALL = pl.ds(0, 2), pl.ds(2, 2), pl.ds(0, 4)
    CL, CR = pl.ds(0, HALF), pl.ds(HALF, HALF)

    def rs1(c, h, e):
        i, j, a, b = first(h)
        return copy(c, 2 * h + e, rows(s.at[c], h, (i + 2) % N, (LOW, HIGH)[e]), r1.at[c, h, e], hop(a, (1, -1)[e]))

    def rs2(c, h, e):
        i, j, a, b = first(h)
        return copy(c, 4 + 2 * h + e, rows(s.at[c], h, (i + (1, 3)[e]) % N, ALL), r2.at[c, h, e], hop(a, (1, -1)[e]))

    def rs4(c, h, e):
        i, j, a, b = first(h)
        return copy(c, 8 + 2 * h + e, rows(s.at[c], h, i, (j + 2) % N).at[:, (CL, CR)[e]], r4.at[c, h, e], hop(b, (1, -1)[e]))

    def rs5(c, h, e):
        i, j, a, b = first(h)
        return copy(c, 12 + 2 * h + e, out5.at[c, h, e], r5.at[c, h, e], hop(b, (1, -1)[e]))

    def ag1(c, h, e, landing=False):
        i, j, a, b = first(h)
        part = rows(s.at[c], h, i, (j + (3, 1)[e]) % N if landing else j)
        return copy(c, 16 + 2 * h + e, part, part, hop(b, (1, -1)[e]))

    def ag2(c, h, e, landing=False):
        i, j, a, b = first(h)
        part = rows(s.at[c], h, i, (j + 2) % N if landing else (j + (3, 1)[e]) % N).at[:, (CL, CR)[e]]
        return copy(c, 20 + 2 * h + e, part, part, hop(b, (1, -1)[e]))

    def ag3(c, h, e, landing=False):
        i, j, a, b = first(h)
        part = rows(s.at[c], h, (i + (3, 1)[e]) % N if landing else i, ALL)
        return copy(c, 24 + 2 * h + e, part, part, hop(a, (1, -1)[e]))

    def ag4(c, h, e, landing=False):
        i, j, a, b = first(h)
        part = rows(s.at[c], h, (i + 2) % N if landing else (i + (3, 1)[e]) % N, (LOW, HIGH)[e])
        return copy(c, 28 + 2 * h + e, part, part, hop(a, (1, -1)[e]))

    BOTH = [(h, e) for e in range(2) for h in range(2)]

    def tile(base, n):
        return pl.ds(pl.multiple_of(base + n * COL, COL), COL)

    def matmul(c):
        rc, base = c % CH, c // CH * PART
        if base not in loaded:
            loaded.add(base)
            load_w(c // CH).wait()
        if ("x", rc) not in loaded:
            loaded.add(("x", rc))
            load_x(rc).wait()

        @pl.loop(0, PART // COL)
        def _(n):
            out = jnp.dot(xv[rc].reshape(ROWS, FEAT), w[:, tile(base, n)], preferred_element_type=F32).astype(BF)
            s[c, :, :, :, :, tile(0, n)] = out.reshape(N, 2, N, TILE, COL)

    def add(dst, src):
        dst[...] = (dst[...].astype(F32) + src[...].astype(F32)).astype(BF)

    def reduce1(c):
        for h, e in BOTH:
            rs1(c, h, e).start()

    def reduce2(c):
        for h, e in BOTH:
            i, j, a, b = first(h)
            rs1(c, h, e).wait_recv()
            f = (i + (1, 3)[e]) % N

            @pl.loop(0, 2)
            def _(g):
                add(rows(s.at[c], h, f, 2 * e + g), r1.at[c, h, e, g])

            rs2(c, h, e).start()

    def reduce3(c):
        for h in range(2):
            i, j, a, b = first(h)
            for e in range(2):
                rs2(c, h, e).wait_recv()

            @pl.loop(0, N)
            def _(g):
                own = rows(s.at[c], h, i, g)
                own[...] = (
                    own[...].astype(F32) + r2[c, h, 0, g].astype(F32) + r2[c, h, 1, g].astype(F32)
                ).astype(BF)

            for e in range(2):
                rs4(c, h, e).start()

    def reduce5(c):
        for make in (rs1, rs2, rs4):
            for h, e in BOTH:
                make(c, h, e).wait_send()
        for h, e in BOTH:
            i, j, a, b = first(h)
            part = rows(s.at[c], h, i, (j + (1, 3)[e]) % N)
            mine, other = ((CL, CR), (CR, CL))[e]
            out5[c, h, e, :, other] = part[:, other]
            rs4(c, h, e).wait_recv()
            out5[c, h, e, :, mine] = (part[:, mine].astype(F32) + r4[c, h, e].astype(F32)).astype(BF)
            rs5(c, h, e).start()

    def reduce6(c):
        for h in range(2):
            i, j, a, b = first(h)
            for e in range(2):
                rs5(c, h, e).wait_recv()
            load_cot(c, h).wait()

            @pl.loop(0, PART // COL)
            def _(n):
                cols = tile(0, n)
                own = rows(s.at[c], h, i, j)
                total = own[:, cols].astype(F32) + r5[c, h, 0, :, cols].astype(F32) + r5[c, h, 1, :, cols].astype(F32)
                pre = total + bias[tile(c // CH * PART, n)][None, :]
                gate = 1.0 / (1.0 + jnp.exp(-pre))
                slope = cot[c, h, :, cols].astype(F32) * gate * (1.0 + pre * (1.0 - gate))
                rows(s.at[c], h, i, j)[:, cols] = slope.astype(BF)

            for e in range(2):
                ag1(c, h, e).start()

    def gather2(c):
        for h, e in BOTH:
            ag1(c, h, e, True).wait_recv()
            ag2(c, h, e).start()

    def gather3(c):
        for h in range(2):
            for e in range(2):
                ag2(c, h, e, True).wait_recv()
            for e in range(2):
                ag3(c, h, e).start()

    def gather4(c):
        for h, e in BOTH:
            ag3(c, h, e, True).wait_recv()
            ag4(c, h, e).start()

    def slot_copy(c, k):
        return pltpu.make_async_remote_copy(
            src_ref=slots.at[c, k], dst_ref=got.at[c, d], send_sem=dp_send.at[c, k], recv_sem=dp_recv.at[c, k],
            device_id=peer(k), device_id_type=MESH,
        )

    def slot_landing(c, k):
        return pltpu.make_async_remote_copy(
            src_ref=slots.at[c, k], dst_ref=got.at[c, (d + DP - k) % DP], send_sem=dp_send.at[c, k],
            recv_sem=dp_recv.at[c, k], device_id=peer(k), device_id_type=MESH,
        )

    def own_slot(c):
        return pltpu.make_async_copy(slots.at[c, 0], got.at[c, d], own_sem.at[c])

    def sent(c):
        for make in (rs5, ag1, ag2, ag3, ag4):
            for h, e in BOTH:
                make(c, h, e).wait_send()

    def landed(c):
        if c not in seen:
            seen.add(c)
            for h, e in BOTH:
                ag4(c, h, e, True).wait_recv()

    def feature_tile(n):
        half = FEAT // 2
        return pl.ds(pl.multiple_of(n * half, half), half)

    def grad_part(c, n):
        cols = pl.ds(c // CH * PART, PART)
        return lax.dot_general(
            s[c].reshape(ROWS, PART), w[feature_tile(n), cols], (((1,), (1,)), ((), ())), preferred_element_type=F32
        )

    def data_grad_left(c):
        landed(c)

        @pl.loop(0, 2)
        def _(n):
            left[:, feature_tile(n)] = grad_part(c, n)

    def data_grad(c):
        landed(c)
        landed(c + CH)

        @pl.loop(0, 2)
        def _(n):
            if ("DL", c) in STEPS:
                out = left[:, feature_tile(n)]
            else:
                out = grad_part(c, n)
            out = (out + grad_part(c + CH, n)).astype(BF)
            gin[:, :, feature_tile(n)] = out.reshape(N, BLOCK, FEAT // 2)

        send_slots(c, FIRST)

    def send_slots(c, which):
        for k in which:
            target = (d + k) % DP
            pick = jnp.int32(0)
            for b in range(1, N):
                pick = jnp.where(owner[b * CH + c] == target, b, pick)
            slots[c, k] = gin[pick]
            if k:
                slot_copy(c, k).start()
            else:
                own_slot(c).start()

    def data_send(c):
        send_slots(c, REST)

    def weight_grad(c):
        landed(c)
        rc, part = c % CH, c // CH
        place = [b for name, b in STEPS if name == "W" and b // CH == part].index(c)
        if rc not in turned:
            turned.add(rc)
            xt[rc] = xv[rc].reshape(ROWS, FEAT).T

        @pl.loop(0, PART // COL)
        def _(n):
            rows_here = s[c, :, :, :, :, tile(0, n)].reshape(ROWS, COL)
            out = jnp.dot(xt[rc], rows_here, preferred_element_type=F32)
            cols = tile(part * PART, n)
            if place == 0:
                acc[:, cols] = out
            elif place < CH - 1:
                acc[:, cols] += out
            else:
                full = ((acc[:, cols] + out) * (float(ROWS * CH * DP) ** -0.5)).astype(BF)
                stage[:, :, :, :, tile(0, n)] = full.reshape(N, 2, N, TILE, COL)

        if place == CH - 1:
            swap(part).start()

    def gw(part, k, src, dst, dev):
        return pltpu.make_async_remote_copy(
            src_ref=src, dst_ref=dst, send_sem=gw_send.at[part, k], recv_sem=gw_recv.at[part, k],
            device_id=dev, device_id_type=MESH,
        )

    def swap(part):
        return gw(part, 0, stage.at[:, 1 - core], pair.at[part], {"dp": 2 * y + 1 - core})

    def ring(e):
        return {"dp": (d + (2, DP - 2)[e]) % DP}

    def ring1(part, e):
        return gw(part, 1 + e, stage.at[(y + 2) % N, core, (LOW, HIGH)[e]], y1.at[part, e], ring(e))

    def ring2(part, e):
        return gw(part, 3 + e, stage.at[(y + (1, 3)[e]) % N, core], y2.at[part, e], ring(e))

    def dp_reduce1(part):
        swap(part).wait_recv()

        @pl.loop(0, N)
        def _(k):
            @pl.loop(0, N)
            def _(g):
                add(stage.at[k, core, g], pair.at[part, k, g])

        for e in range(2):
            ring1(part, e).start()

    def dp_reduce2(part):
        for e in range(2):
            ring1(part, e).wait_recv()

            @pl.loop(0, 2)
            def _(g):
                add(stage.at[(y + (1, 3)[e]) % N, core, 2 * e + g], y1.at[part, e, g])

            ring2(part, e).start()

    def dp_reduce3(part):
        for e in range(2):
            ring2(part, e).wait_recv()

        @pl.loop(0, N)
        def _(g):
            grad_out[g, :, pl.ds(part * PART, PART)] = (
                stage[y, core, g].astype(F32) + y2[part, 0, g].astype(F32) + y2[part, 1, g].astype(F32)
            )

        swap(part).wait_send()
        for e in range(2):
            ring1(part, e).wait_send()
            ring2(part, e).wait_send()

    def info_copy(k):
        return pltpu.make_async_remote_copy(
            src_ref=info, dst_ref=got_info.at[d], send_sem=info_send.at[k], recv_sem=info_recv.at[k],
            device_id=peer(k), device_id_type=MESH,
        )

    def info_landing(k):
        return pltpu.make_async_remote_copy(
            src_ref=info, dst_ref=got_info.at[(d + DP - k) % DP], send_sem=info_send.at[k], recv_sem=info_recv.at[k],
            device_id=peer(k), device_id_type=MESH,
        )

    own_info = pltpu.make_async_copy(info, got_info.at[d], info_send.at[0])

    phases = {
        "A": matmul, "R1": reduce1, "R2": reduce2, "R3": reduce3, "R5": reduce5, "R6": reduce6,
        "G2": gather2, "G3": gather3, "G4": gather4, "DL": data_grad_left, "D": data_grad, "E": data_send,
        "W": weight_grad, "Y1": dp_reduce1, "Y2": dp_reduce2, "Y3": dp_reduce3,
    }
    seen, turned, loaded = set(), set(), set()
    phases[STEPS[0][0]](STEPS[0][1])
    pl.semaphore_wait(barrier, 4 + DP - 1)
    phases[STEPS[1][0]](STEPS[1][1])
    own_info.start()
    for k in range(1, DP):
        info_copy(k).start()
    for name, c in STEPS[2:]:
        phases[name](c)

    own_info.wait()
    for k in range(1, DP):
        info_copy(k).wait_send()
        info_landing(k).wait_recv()
    for c in range(ALL_CH):
        sent(c)
    for c in range(CH):
        own_slot(c).wait()
        for k in range(1, DP):
            slot_copy(c, k).wait_send()
            slot_landing(c, k).wait_recv()


def place_kernel(me, info, got, grad, out, grad_out, table, held, zeros, passed, flag, info_sem, in_sem, grad_sem, out_sem):
    fetch = pltpu.make_async_copy(info, table, info_sem)
    fetch.start()
    loads = [pltpu.make_async_copy(got.at[c], held.at[c], in_sem.at[c]) for c in range(CH)]
    for load in loads:
        load.start()
    take = pltpu.make_async_copy(grad, passed, grad_sem)
    take.start()
    zeros[...] = jnp.zeros_like(zeros)
    count = out.shape[0]
    for j in range(count):
        flag[j] = 0
    fetch.wait()
    give = pltpu.make_async_copy(passed, grad_out, grad_sem)
    mine = me[0]
    for c in range(CH):
        loads[c].wait()
        for source in range(DP):
            for b in range(N):

                @pl.when(table[source, 0, b * CH + c] == mine)
                def _():
                    row = table[source, 1, b * CH + c]
                    flag[row] = 1
                    pltpu.make_async_copy(held.at[c, source], out.at[row], out_sem).start()

    take.wait()
    give.start()
    for j in range(count):

        @pl.when(flag[j] == 0)
        def _():
            pltpu.make_async_copy(zeros, out.at[j], out_sem).start()

    pltpu.make_async_copy(out, out, out_sem).wait()
    give.wait()


def shards(thinker_rows, proj_weight, proj_bias, cotangent, block_owner, block_offset):
    vmem = pl.BlockSpec(memory_space=pltpu.VMEM)
    smem = pl.BlockSpec(memory_space=pltpu.SMEM)
    hbm = pl.BlockSpec(memory_space=pl.ANY)
    tile = (TILE, PART)
    row = (TILE, WIDTH)
    dma = pltpu.SemaphoreType.DMA
    got, got_info, grad = pl.pallas_call(
        main_kernel,
        out_shape=(
            jax.ShapeDtypeStruct((CH, DP, BLOCK, FEAT), BF),
            jax.ShapeDtypeStruct((DP, 8, 128), jnp.int32),
            jax.ShapeDtypeStruct((N,) + row, F32),
        ),
        in_specs=[smem, smem, vmem, hbm, hbm, hbm],
        out_specs=(hbm, hbm, vmem),
        scratch_shapes=[
            pltpu.VMEM((8, 128), jnp.int32),
            pltpu.VMEM((CH, N, BLOCK, FEAT), BF),
            pltpu.VMEM((CH, FEAT, ROWS), BF),
            pltpu.VMEM((FEAT, WIDTH), BF),
            pltpu.VMEM((ALL_CH, N, 2, N) + tile, BF),
            pltpu.VMEM((ALL_CH, 2, 2, 2) + tile, BF),
            pltpu.VMEM((ALL_CH, 2, 2, N) + tile, BF),
            pltpu.VMEM((ALL_CH, 2, 2, TILE, HALF), BF),
            pltpu.VMEM((ALL_CH, 2, 2) + tile, BF),
            pltpu.VMEM((ALL_CH, 2, 2) + tile, BF),
            pltpu.VMEM((ALL_CH, 2) + tile, BF),
            pltpu.VMEM((FEAT, WIDTH), F32),
            pltpu.VMEM((ROWS, FEAT), F32),
            pltpu.VMEM((N, BLOCK, FEAT), BF),
            pltpu.VMEM((CH, DP, BLOCK, FEAT), BF),
            pltpu.VMEM((N, 2, N) + tile, BF),
            pltpu.VMEM((PARTS, N, N) + tile, BF),
            pltpu.VMEM((PARTS, 2, 2) + tile, BF),
            pltpu.VMEM((PARTS, 2, N) + tile, BF),
            dma((CH + PARTS,)),
            dma((ALL_CH, 2)),
            dma((ALL_CH, 32)),
            dma((ALL_CH, 32)),
            dma((CH, DP)),
            dma((CH, DP)),
            dma((CH,)),
            dma((DP,)),
            dma((DP,)),
            dma((PARTS, 5)),
            dma((PARTS, 5)),
        ],
        compiler_params=pltpu.CompilerParams(
            collective_id=0, has_side_effects=True, vmem_limit_bytes=67_000_000
        ),
        name="fused_backward",
    )(
        block_owner,
        block_offset,
        proj_bias,
        thinker_rows.reshape(N, CH, BLOCK, FEAT),
        proj_weight,
        cotangent.reshape(N, CH, 2, N, TILE, WIDTH),
    )
    placed, grad = pl.pallas_call(
        place_kernel,
        out_shape=(
            jax.ShapeDtypeStruct((CH * DP, BLOCK, FEAT), BF),
            jax.ShapeDtypeStruct((N,) + row, F32),
        ),
        in_specs=[smem, hbm, hbm, hbm],
        out_specs=(hbm, hbm),
        scratch_shapes=[
            pltpu.SMEM((DP, 8, 128), jnp.int32),
            pltpu.VMEM((CH, DP, BLOCK, FEAT), BF),
            pltpu.VMEM((BLOCK, FEAT), BF),
            pltpu.VMEM((N,) + row, F32),
            pltpu.SMEM((CH * DP,), jnp.int32),
            dma,
            dma((CH,)),
            dma,
            dma,
        ],
        name="place_blocks",
    )(lax.axis_index("dp").reshape(1), got_info, got, grad)
    return (placed.reshape(CH * DP * BLOCK, FEAT), grad.reshape(N * TILE, WIDTH))


def solution(mesh):
    return jax.shard_map(
        shards,
        mesh=mesh,
        in_specs=(P("dp", "tensor"), P("tensor", None), P(), P("dp", None), P("dp"), P("dp")),
        out_specs=(P("dp", "tensor"), P(("tensor", "dp"), None)),
        check_vma=False,
    )
```
